32 devices in a mesh: ctx: 16 (over z, y, core), fsdp: 2 (over x).
Axes of the slice: x: 2, y: 2, z: 4, core: 2. Of those that a mesh axis runs over, the one named last changes fastest.
Arguments:
- outer_gate: bfloat16 [8192, 2048], P('ctx', 'fsdp'), may hold values from -6 to 6
- inner_gate: bfloat16 [8192, 2048], P('ctx', 'fsdp'), may hold values from -6 to 6
- values: bfloat16 [8192, 2048], P('ctx', 'fsdp'), may hold values from -6 to 6
- out_weight: bfloat16 [2048, 2048], P('ctx', 'fsdp'), may hold values from -0.125 to 0.125
- skip_gain: float32 [2048], P('fsdp'), may hold values from 0.25 to 1.5
- residues: float32 [2048, 16], P('fsdp')
- decay_rates: float32 [2048, 16], P('fsdp')
- out_grad: bfloat16 [8192, 2048], P('ctx', 'fsdp'), may hold values from -6 to 6
Outputs:
- block_out: bfloat16 [8192, 2048], P('ctx', 'fsdp')
- outer_grad: bfloat16 [8192, 2048], P('ctx', 'fsdp')
- inner_grad: bfloat16 [8192, 2048], P('ctx', 'fsdp')
- value_grad: bfloat16 [8192, 2048], P('ctx', 'fsdp')
- weight_grad: float32 [2048, 2048], P('ctx', 'fsdp')
The draws below stay inside these ranges and needn't reach their ends.
All inputs are finite; a program needn't handle non-finite values.
Results may differ from the reference program's by a relative error of at most 0.011.
Values may be sent and summed in bfloat16 or wider, within the bound.
A program may use at most 192 MiB of HBM per device.

```python
import math
import jax
import jax.numpy as jnp
from jax import lax

WIDTH = 2048
FEATURES = 2048
MODES = 16
LENGTH = 8192
N_FSDP = 2


def mode_pair(key):
    folded = jax.random.fold_in(key, 11)
    pick_key, slow_key, fast_key, spread_key = jax.random.split(folded, 4)
    slow_share = 0.5
    chosen = jax.random.uniform(pick_key, (WIDTH, MODES), jnp.float32) < slow_share
    slow_rates = jnp.exp(jax.random.uniform(slow_key, (WIDTH, MODES), jnp.float32, minval=math.log(0.2 / LENGTH), maxval=math.log(2.0 / LENGTH)))
    fast_rates = jnp.exp(jax.random.uniform(fast_key, (WIDTH, MODES), jnp.float32, minval=math.log(1.0 / 50.0), maxval=math.log(1.0 / 30.0)))
    all_rates = jnp.where(chosen, slow_rates, fast_rates)
    spread = jnp.clip(jax.random.normal(spread_key, (WIDTH, MODES), jnp.float32), -3.0, 3.0)
    residue = spread * jnp.sqrt(2.0 * all_rates / MODES)
    return (all_rates, residue)


def draw_decay_rates(key, part):
    return mode_pair(key)[0]


def draw_residues(key, part):
    return mode_pair(key)[1]


def block_scale(rng, extent, shards, least, high):
    level, own = 1.0, jax.random.fold_in(rng, 6)
    for axis_at, blocks in shards:
        steps = jnp.exp(jax.random.uniform(jax.random.fold_in(own, axis_at), (blocks,), jnp.float32, least / len(shards), high / len(shards)))
        level = level * jnp.repeat(steps, extent[axis_at] // blocks).reshape([-1 if axis == axis_at else 1 for axis in range(len(extent))])
    return level


def noise(stream_key, extent, deviation, most, shards=(), kind=jnp.bfloat16):
    factor_of = block_scale(stream_key, extent, shards, -0.22, 0.18) if shards else 1.0
    array = jax.random.normal(stream_key, extent, jnp.float32) * deviation * factor_of
    return jnp.minimum(jnp.maximum(array, -most), most).astype(kind)


def setup_inputs(seed: int = 0) -> dict:
    keys = jax.random.split(jax.random.key(seed), 9)
    outer_gate = noise(keys[0], (LENGTH, WIDTH), 1.0, 6.0, ((0, 16), (1, 2)))
    inner_gate = noise(keys[1], (LENGTH, WIDTH), 1.0, 6.0, ((0, 16), (1, 2)))
    values = noise(keys[2], (LENGTH, WIDTH), 1.0, 6.0, ((0, 16), (1, 2)))
    out_weight = noise(keys[3], (WIDTH, FEATURES), WIDTH ** -0.5, 0.125, ((0, 16), (1, 2)))
    skip_gain = jnp.clip(0.25 + 1.25 * jax.random.uniform(keys[4], (WIDTH,), jnp.float32) ** block_scale(keys[4], (WIDTH,), ((0, 2),), -0.2, 0.2), 0.25, 1.5)
    residues = draw_residues(jax.random.fold_in(keys[8], 71), 0)
    decay_rates = draw_decay_rates(jax.random.fold_in(keys[8], 71), 0)
    out_grad = noise(keys[7], (LENGTH, FEATURES), 1.0, 6.0, ((0, 16), (1, 2)))
    return dict(outer_gate=outer_gate, inner_gate=inner_gate, values=values, out_weight=out_weight, skip_gain=skip_gain, residues=residues, decay_rates=decay_rates, out_grad=out_grad)


def mode_tables(residues, decay_rates, row_count):
    block_rows = min(64, row_count)
    lag_steps = jnp.arange(block_rows, dtype=jnp.float32)
    lag_index = jnp.arange(block_rows)[:, None] - jnp.arange(block_rows)[None, :]
    kernel = lax.optimization_barrier(jnp.sum(residues[:, :, None] * jnp.exp(-decay_rates[:, :, None] * lag_steps[None, None, :]), axis=1))
    picked = kernel[:, jnp.clip(lag_index, 0, block_rows - 1)]
    toeplitz = jnp.where((lag_index >= 0)[None], picked, jnp.zeros_like(picked))
    rise_table = jnp.exp(-decay_rates[None] * (lag_steps[:, None, None] + 1.0))
    tail_table = jnp.exp(-decay_rates[None] * (block_rows - 1.0 - lag_steps)[:, None, None])
    return (block_rows, toeplitz, rise_table, tail_table)

def local_forward(inputs, decay_rates, tables):
    block_rows, toeplitz, rise_table, tail_table = tables
    blocks = inputs.shape[0] // block_rows
    shaped = inputs.reshape(blocks, block_rows, inputs.shape[1])
    inner_part = jnp.einsum('cts,nsc->ntc', toeplitz, shaped, precision=lax.Precision.HIGHEST)
    end_terms = jnp.einsum('nsc,scr->ncr', shaped, tail_table, precision=lax.Precision.HIGHEST)
    step_decay = jnp.exp(-decay_rates * block_rows)

    def advance(running, end_term):
        return (step_decay * running + end_term, running)
    end_state, befores = lax.scan(advance, jnp.zeros(decay_rates.shape, jnp.float32), end_terms)
    return (inner_part, befores, end_state)

def finish_forward(inner_part, befores, incoming, residues, decay_rates, tables):
    block_rows, toeplitz, rise_table, tail_table = tables
    blocks = inner_part.shape[0]
    offsets = block_rows * jnp.arange(blocks, dtype=jnp.float32)
    powers = jnp.exp(-decay_rates[None] * offsets[:, None, None])
    states = befores + powers * incoming[None]
    cross_part = jnp.einsum('tcr,ncr->ntc', rise_table * residues[None], states, precision=lax.Precision.HIGHEST)
    total = inner_part + cross_part
    return total.reshape(blocks * block_rows, total.shape[2])

def local_backward(grads, decay_rates, tables):
    block_rows, toeplitz, rise_table, tail_table = tables
    blocks = grads.shape[0] // block_rows
    shaped = grads.reshape(blocks, block_rows, grads.shape[1])
    inner_part = jnp.einsum('cts,ntc->nsc', toeplitz, shaped, precision=lax.Precision.HIGHEST)
    start_terms = jnp.einsum('ntc,tcr->ncr', shaped, rise_table, precision=lax.Precision.HIGHEST)
    step_decay = jnp.exp(-decay_rates * block_rows)

    def retreat(running, start_term):
        return (step_decay * running + start_term, running)
    start_state, afters = lax.scan(retreat, jnp.zeros(decay_rates.shape, jnp.float32), start_terms, reverse=True)
    return (inner_part, afters, start_state)

def finish_backward(inner_part, afters, outgoing, residues, decay_rates, tables):
    block_rows, toeplitz, rise_table, tail_table = tables
    blocks = inner_part.shape[0]
    offsets = block_rows * (blocks - 1.0 - jnp.arange(blocks, dtype=jnp.float32))
    powers = jnp.exp(-decay_rates[None] * offsets[:, None, None])
    states = afters + powers * outgoing[None]
    cross_part = jnp.einsum('scr,ncr->nsc', tail_table * residues[None], states, precision=lax.Precision.HIGHEST)
    total = inner_part + cross_part
    return total.reshape(blocks * block_rows, total.shape[2])

def reference(outer_gate, inner_gate, values, out_weight, skip_gain, residues, decay_rates, out_grad):
    row_count = outer_gate.shape[0]
    tables = mode_tables(residues, decay_rates, row_count)
    zero_state = jnp.zeros(decay_rates.shape, jnp.float32)
    gated = inner_gate.astype(jnp.float32) * values.astype(jnp.float32)
    inner_part, befores, end_state = local_forward(gated, decay_rates, tables)
    filtered = finish_forward(inner_part, befores, zero_state, residues, decay_rates, tables) + skip_gain[None] * gated
    modulated = (outer_gate.astype(jnp.float32) * filtered).astype(jnp.bfloat16)
    block_out = jnp.dot(modulated, out_weight, preferred_element_type=jnp.float32).astype(jnp.bfloat16)
    block_cols = FEATURES // N_FSDP
    modulated_grad = jnp.zeros(modulated.shape, jnp.float32)
    for member in range(N_FSDP):
        first_col = member * block_cols
        partial_term = jnp.dot(out_grad[:, first_col:first_col + block_cols], out_weight[:, first_col:first_col + block_cols].T, preferred_element_type=jnp.float32)
        rounded = lax.optimization_barrier(partial_term.astype(jnp.bfloat16))
        modulated_grad = modulated_grad + rounded.astype(jnp.float32)
    outer_grad = (modulated_grad * filtered).astype(jnp.bfloat16)
    filtered_grad = modulated_grad * outer_gate.astype(jnp.float32)
    inner_back, afters, start_state = local_backward(filtered_grad, decay_rates, tables)
    gated_grad = finish_backward(inner_back, afters, zero_state, residues, decay_rates, tables) + skip_gain[None] * filtered_grad
    inner_grad = (gated_grad * values.astype(jnp.float32)).astype(jnp.bfloat16)
    value_grad = (gated_grad * inner_gate.astype(jnp.float32)).astype(jnp.bfloat16)
    weight_grad = jnp.dot(modulated.T, out_grad, preferred_element_type=jnp.float32) * (1.0 / math.sqrt(LENGTH))
    return (block_out, outer_grad, inner_grad, value_grad, weight_grad)
```

```python
import functools
import math

import jax
import jax.numpy as jnp
from jax import lax
from jax.experimental import pallas as pl
from jax.experimental.pallas import tpu as pltpu
from jax.sharding import PartitionSpec as P

F32 = jnp.float32
BF16 = jnp.bfloat16
LANES = 128
SEGS = 8


def rows_at(i, steps):
    return pl.ds(i, SEGS, stride=steps)


def spread(row):
    return jnp.broadcast_to(row, (SEGS, LANES))


def segment_states(u_scr, decay_ref, pre_ref, end_ref, reverse):
    modes = decay_ref.shape[0]
    steps = u_scr.shape[0] // SEGS
    a = [spread(jnp.exp(-decay_ref[r : r + 1, :])) for r in range(modes)]

    def step(k, states):
        i = steps - 1 - k if reverse else k
        u = u_scr[rows_at(i, steps), :]
        return tuple(a[r] * states[r] + u for r in range(modes))

    zero = jnp.zeros((SEGS, LANES), F32)
    states = lax.fori_loop(0, steps, step, (zero,) * modes, unroll=4)
    seg = lax.broadcasted_iota(jnp.int32, (SEGS, LANES), 0)

    def moved(x, by):
        if reverse:
            return jnp.where(seg < SEGS - by, pltpu.roll(x, SEGS - by, 0), 0.0)
        return jnp.where(seg >= by, pltpu.roll(x, by, 0), 0.0)

    last = 0 if reverse else SEGS - 1
    for r in range(modes):
        rate = spread(decay_ref[r : r + 1, :])
        x = states[r]
        for by in (1, 2, 4):
            x = x + jnp.exp(-rate * float(steps * by)) * moved(x, by)
        end_ref[r : r + 1, :] = x[last : last + 1, :]
        pre_ref[r] = moved(x, 1)


def full_scan(u_scr, y_scr, decay_ref, res_ref, pre_ref, ends_ref, reverse):
    modes = decay_ref.shape[0]
    rows = u_scr.shape[0]
    steps = rows // SEGS
    ctx = ends_ref.shape[0]
    me = lax.axis_index("ctx")
    whole = jnp.exp(-decay_ref[...] * float(rows))

    def add_device(k, incoming):
        j = ctx - 1 - k if reverse else k
        before = j > me if reverse else j < me
        return jnp.where(before, whole * incoming + ends_ref[j], incoming)

    incoming = lax.fori_loop(0, ctx, add_device, jnp.zeros(decay_ref.shape, F32))
    seg = lax.broadcasted_iota(jnp.int32, (SEGS, LANES), 0)
    ahead = ((SEGS - 1 - seg if reverse else seg) * steps).astype(F32)
    a = []
    first = []
    for r in range(modes):
        rate = spread(decay_ref[r : r + 1, :])
        a.append(jnp.exp(-rate))
        first.append(pre_ref[r] + jnp.exp(-rate * ahead) * incoming[r : r + 1, :])
    res = [spread(res_ref[r : r + 1, :]) for r in range(modes)]

    def step(k, states):
        i = steps - 1 - k if reverse else k
        u = u_scr[rows_at(i, steps), :]
        states = tuple(a[r] * states[r] + u for r in range(modes))
        terms = [res[r] * states[r] for r in range(modes)]
        while len(terms) > 1:
            terms = [p + q for p, q in zip(terms[::2], terms[1::2])]
        y_scr[rows_at(i, steps), :] = terms[0]
        return states

    lax.fori_loop(0, steps, step, tuple(first), unroll=2)


def forward_ends(inner_ref, values_ref, decay_ref, pre_ref, end_ref, u_scr):
    u_scr[...] = inner_ref[...].astype(F32) * values_ref[...].astype(F32)
    segment_states(u_scr, decay_ref, pre_ref, end_ref, False)


def forward_finish(
    inner_ref, values_ref, outer_ref, decay_ref, res_ref, skip_ref, pre_ref, ends_ref,
    filtered_ref, modulated_ref, u_scr, y_scr,
):
    u_scr[...] = inner_ref[...].astype(F32) * values_ref[...].astype(F32)
    full_scan(u_scr, y_scr, decay_ref, res_ref, pre_ref, ends_ref, False)
    filtered = y_scr[...] + skip_ref[...] * u_scr[...]
    filtered_ref[...] = filtered
    modulated_ref[...] = (outer_ref[...].astype(F32) * filtered).astype(BF16)


def backward_ends(grad_ref, outer_ref, decay_ref, pre_ref, end_ref, u_scr):
    u_scr[...] = grad_ref[...].astype(F32) * outer_ref[...].astype(F32)
    segment_states(u_scr, decay_ref, pre_ref, end_ref, True)


def backward_finish(
    grad_ref, outer_ref, inner_ref, values_ref, filtered_ref, decay_ref, res_ref, skip_ref,
    pre_ref, ends_ref, outer_grad_ref, inner_grad_ref, value_grad_ref, u_scr, y_scr,
):
    grad = grad_ref[...].astype(F32)
    u_scr[...] = grad * outer_ref[...].astype(F32)
    outer_grad_ref[...] = (grad * filtered_ref[...]).astype(BF16)
    full_scan(u_scr, y_scr, decay_ref, res_ref, pre_ref, ends_ref, True)
    gated_grad = y_scr[...] + skip_ref[...] * u_scr[...]
    inner_grad_ref[...] = (gated_grad * values_ref[...].astype(F32)).astype(BF16)
    value_grad_ref[...] = (gated_grad * inner_ref[...].astype(F32)).astype(BF16)


def by_lanes(kernel, operands, outs, rows, scans):
    channels = operands[0].shape[-1]

    def spec(x):
        lead = x.shape[:-1]
        return pl.BlockSpec(lead + (LANES,), lambda c, n=len(lead): (0,) * n + (c,))

    work = rows * channels * 16 * (6 if scans > 1 else 2)
    moved = sum(math.prod(x.shape) * x.dtype.itemsize for x in list(operands) + list(outs))
    return pl.pallas_call(
        kernel,
        grid=(channels // LANES,),
        out_shape=outs,
        in_specs=[spec(x) for x in operands],
        out_specs=[spec(x) for x in outs],
        scratch_shapes=[pltpu.VMEM((rows, LANES), F32)] * scans,
        cost_estimate=pl.CostEstimate(flops=work, bytes_accessed=moved, transcendentals=0),
        name=kernel.__name__,
    )(*operands)


def shards(outer_gate, inner_gate, values, out_weight, skip_gain, residues, decay_rates, out_grad):
    rows, channels = values.shape
    modes = decay_rates.shape[1]
    ctx = lax.axis_size("ctx")
    shape = jax.ShapeDtypeStruct
    panel = lax.all_gather(out_weight, "ctx", axis=0, tiled=True)
    decay = decay_rates.T
    res = residues.T
    skip = skip_gain[None]
    state_outs = [shape((modes, SEGS, channels), F32), shape((modes, channels), F32)]
    pre, end = by_lanes(forward_ends, (inner_gate, values, decay), state_outs, rows, 1)
    ends = lax.all_gather(end, "ctx", axis=0)
    filtered, modulated = by_lanes(
        forward_finish,
        (inner_gate, values, outer_gate, decay, res, skip, pre, ends),
        [shape((rows, channels), F32), shape((rows, channels), BF16)],
        rows,
        2,
    )
    gathered = lax.all_gather(modulated, "fsdp", axis=1, tiled=True)
    grad_rows = lax.dot_general(
        gathered, out_grad, (((0,), (0,)), ((), ())), preferred_element_type=F32
    ).astype(BF16)
    weight_grad = lax.psum_scatter(grad_rows, "ctx", scatter_dimension=0, tiled=True)
    weight_grad = weight_grad.astype(F32) * (1.0 / math.sqrt(rows * ctx))
    block_out = jnp.dot(gathered, panel, preferred_element_type=F32).astype(BF16)
    partial = jnp.dot(out_grad, panel.T, preferred_element_type=F32).astype(BF16)
    grad = lax.psum_scatter(partial, "fsdp", scatter_dimension=1, tiled=True)
    pre, end = by_lanes(backward_ends, (grad, outer_gate, decay), state_outs, rows, 1)
    ends = lax.all_gather(end, "ctx", axis=0)
    outer_grad, inner_grad, value_grad = by_lanes(
        backward_finish,
        (grad, outer_gate, inner_gate, values, filtered, decay, res, skip, pre, ends),
        [shape((rows, channels), BF16)] * 3,
        rows,
        2,
    )
    return (block_out, outer_grad, inner_grad, value_grad, weight_grad)


def solution(mesh):
    tile = P("ctx", "fsdp")
    return jax.shard_map(
        shards,
        mesh=mesh,
        in_specs=(tile, tile, tile, tile, P("fsdp"), P("fsdp", None), P("fsdp", None), tile),
        out_specs=(tile,) * 5,
        check_vma=False,
    )
```

```python
import functools
import math

import jax
import jax.numpy as jnp
from jax import lax
from jax.experimental import pallas as pl
from jax.experimental.pallas import tpu as pltpu
from jax.sharding import PartitionSpec as P

F32 = jnp.float32
BF16 = jnp.bfloat16
LANES = 128
SEGS = 8


def rows_at(i, steps):
    return pl.ds(i, SEGS, stride=steps)


def spread(row):
    return jnp.broadcast_to(row, (SEGS, LANES))


def segment_states(u_scr, decay_ref, pre_ref, end_ref, reverse):
    modes = decay_ref.shape[0]
    steps = u_scr.shape[0] // SEGS
    a = [spread(jnp.exp(-decay_ref[r : r + 1, :])) for r in range(modes)]

    def step(k, states):
        i = steps - 1 - k if reverse else k
        u = u_scr[rows_at(i, steps), :]
        return tuple(a[r] * states[r] + u for r in range(modes))

    zero = jnp.zeros((SEGS, LANES), F32)
    states = lax.fori_loop(0, steps, step, (zero,) * modes, unroll=4)
    seg = lax.broadcasted_iota(jnp.int32, (SEGS, LANES), 0)

    def moved(x, by):
        if reverse:
            return jnp.where(seg < SEGS - by, pltpu.roll(x, SEGS - by, 0), 0.0)
        return jnp.where(seg >= by, pltpu.roll(x, by, 0), 0.0)

    last = 0 if reverse else SEGS - 1
    for r in range(modes):
        rate = spread(decay_ref[r : r + 1, :])
        x = states[r]
        for by in (1, 2, 4):
            x = x + jnp.exp(-rate * float(steps * by)) * moved(x, by)
        end_ref[r : r + 1, :] = x[last : last + 1, :]
        pre_ref[r] = moved(x, 1)


def full_scan(u_scr, y_scr, decay_ref, res_ref, pre_ref, incoming_ref, reverse):
    modes = decay_ref.shape[0]
    rows = u_scr.shape[0]
    steps = rows // SEGS
    seg = lax.broadcasted_iota(jnp.int32, (SEGS, LANES), 0)
    ahead = ((SEGS - 1 - seg if reverse else seg) * steps).astype(F32)
    a = []
    first = []
    for r in range(modes):
        rate = spread(decay_ref[r : r + 1, :])
        a.append(jnp.exp(-rate))
        first.append(pre_ref[r] + jnp.exp(-rate * ahead) * incoming_ref[r : r + 1, :])
    res = [spread(res_ref[r : r + 1, :]) for r in range(modes)]

    def step(k, states):
        i = steps - 1 - k if reverse else k
        u = u_scr[rows_at(i, steps), :]
        states = tuple(a[r] * states[r] + u for r in range(modes))
        terms = [res[r] * states[r] for r in range(modes)]
        while len(terms) > 1:
            terms = [p + q for p, q in zip(terms[::2], terms[1::2])]
        y_scr[rows_at(i, steps), :] = terms[0]
        return states

    lax.fori_loop(0, steps, step, tuple(first), unroll=2)


def forward_ends(inner_ref, values_ref, decay_ref, pre_ref, end_ref, u_scr):
    u_scr[...] = inner_ref[...].astype(F32) * values_ref[...].astype(F32)
    segment_states(u_scr, decay_ref, pre_ref, end_ref, False)


def forward_finish(
    inner_ref, values_ref, outer_ref, decay_ref, res_ref, skip_ref, pre_ref, incoming_ref,
    filtered_ref, modulated_ref, u_scr, y_scr,
):
    u_scr[...] = inner_ref[...].astype(F32) * values_ref[...].astype(F32)
    full_scan(u_scr, y_scr, decay_ref, res_ref, pre_ref, incoming_ref, False)
    filtered = y_scr[...] + skip_ref[...] * u_scr[...]
    filtered_ref[...] = filtered
    modulated_ref[...] = (outer_ref[...].astype(F32) * filtered).astype(BF16)


def backward_ends(own_ref, other_ref, outer_ref, decay_ref, pre_ref, end_ref, u_scr):
    grad = own_ref[...].astype(F32) + other_ref[...].astype(F32)
    u_scr[...] = grad * outer_ref[...].astype(F32)
    segment_states(u_scr, decay_ref, pre_ref, end_ref, True)


def backward_finish(
    own_ref, other_ref, outer_ref, inner_ref, values_ref, filtered_ref, decay_ref, res_ref, skip_ref,
    pre_ref, incoming_ref, outer_grad_ref, inner_grad_ref, value_grad_ref, u_scr, y_scr,
):
    grad = own_ref[...].astype(F32) + other_ref[...].astype(F32)
    u_scr[...] = grad * outer_ref[...].astype(F32)
    outer_grad_ref[...] = (grad * filtered_ref[...]).astype(BF16)
    full_scan(u_scr, y_scr, decay_ref, res_ref, pre_ref, incoming_ref, True)
    gated_grad = y_scr[...] + skip_ref[...] * u_scr[...]
    inner_grad_ref[...] = (gated_grad * values_ref[...].astype(F32)).astype(BF16)
    value_grad_ref[...] = (gated_grad * inner_ref[...].astype(F32)).astype(BF16)


def by_lanes(kernel, operands, outs, rows, scans):
    channels = operands[0].shape[-1]

    def spec(x):
        lead = x.shape[:-1]
        return pl.BlockSpec(lead + (LANES,), lambda c, n=len(lead): (0,) * n + (c,))

    work = rows * channels * 16 * (6 if scans > 1 else 2)
    moved = sum(math.prod(x.shape) * x.dtype.itemsize for x in list(operands) + list(outs))
    return pl.pallas_call(
        kernel,
        grid=(channels // LANES,),
        out_shape=outs,
        in_specs=[spec(x) for x in operands],
        out_specs=[spec(x) for x in outs],
        scratch_shapes=[pltpu.VMEM((rows, LANES), F32)] * scans,
        cost_estimate=pl.CostEstimate(flops=work, bytes_accessed=moved, transcendentals=0),
        name=kernel.__name__,
    )(*operands)


def prefix_kernel(reverse, rows, end_ref, decay_ref, out_ref, sent, got, send_sem, recv_sem):
    me, n = lax.axis_index("ctx"), lax.axis_size("ctx")
    hops = [1 << k for k in range(sent.shape[0])]
    barrier = pltpu.get_barrier_semaphore()
    for hop in hops:
        for peer in (lax.rem(me + hop, n), lax.rem(me + n - hop, n)):
            pl.semaphore_signal(
                barrier, inc=1, device_id={"ctx": peer}, device_id_type=pl.DeviceIdType.MESH
            )
    pl.semaphore_wait(barrier, 2 * len(hops))
    decay = decay_ref[...]
    upto = end_ref[...]
    before = jnp.zeros_like(upto)
    for k, hop in enumerate(hops):
        sent[k] = upto
        copy = pltpu.make_async_remote_copy(
            src_ref=sent.at[k],
            dst_ref=got.at[k],
            send_sem=send_sem.at[k],
            recv_sem=recv_sem.at[k],
            device_id={"ctx": lax.rem(me + (n - hop if reverse else hop), n)},
            device_id_type=pl.DeviceIdType.MESH,
        )
        copy.start()
        near = jnp.exp(-decay * float(rows * (hop - 1)))
        far = jnp.exp(-decay * float(rows * hop))
        copy.wait()
        inside = (me + hop < n) if reverse else (me >= hop)
        term = got[k] * jnp.where(inside, 1.0, 0.0)
        before = before + near * term
        upto = upto + far * term
    out_ref[...] = before


def prefix(end, decay, rows, reverse):
    hops = max(1, (lax.axis_size("ctx") - 1).bit_length())
    whole = pl.BlockSpec(memory_space=pltpu.VMEM)
    return pl.pallas_call(
        functools.partial(prefix_kernel, reverse, rows),
        out_shape=jax.ShapeDtypeStruct(end.shape, F32),
        in_specs=[whole, whole],
        out_specs=whole,
        scratch_shapes=[
            pltpu.VMEM((hops,) + end.shape, F32),
            pltpu.VMEM((hops,) + end.shape, F32),
            pltpu.SemaphoreType.DMA((hops,)),
            pltpu.SemaphoreType.DMA((hops,)),
        ],
        compiler_params=pltpu.CompilerParams(
            collective_id=2 if reverse else 1, has_side_effects=True
        ),
        name="prefix_back" if reverse else "prefix_ahead",
    )(end, decay)


def shards(outer_gate, inner_gate, values, out_weight, skip_gain, residues, decay_rates, out_grad):
    rows, channels = values.shape
    modes = decay_rates.shape[1]
    ctx, fsdp = lax.axis_size("ctx"), lax.axis_size("fsdp")
    at = lax.axis_index("fsdp")
    swap = [(0, 1), (1, 0)]
    shape = jax.ShapeDtypeStruct
    panel = lax.all_gather(out_weight, "ctx", axis=0, tiled=True)
    decay = decay_rates.T
    res = residues.T
    skip = skip_gain[None]
    state_outs = [shape((modes, SEGS, channels), F32), shape((modes, channels), F32)]
    pre, end = by_lanes(forward_ends, (inner_gate, values, decay), state_outs, rows, 1)
    incoming = prefix(end, decay, rows, False)
    filtered, modulated = by_lanes(
        forward_finish,
        (inner_gate, values, outer_gate, decay, res, skip, pre, incoming),
        [shape((rows, channels), F32), shape((rows, channels), BF16)],
        rows,
        2,
    )
    if fsdp == 2:
        other = lax.ppermute(modulated, "fsdp", swap)
        first = jnp.where(at == 0, modulated, other)
        second = jnp.where(at == 0, other, modulated)
        gathered = jnp.concatenate([first, second], axis=1)
        mine = lax.dynamic_slice_in_dim(panel, at * channels, channels, 0)
        theirs = lax.dynamic_slice_in_dim(panel, (1 - at) * channels, channels, 0)
        for_them = jnp.dot(out_grad, theirs.T, preferred_element_type=F32).astype(BF16)
        from_them = lax.ppermute(for_them, "fsdp", swap)
        own = jnp.dot(out_grad, mine.T, preferred_element_type=F32).astype(BF16)
    else:
        gathered = lax.all_gather(modulated, "fsdp", axis=1, tiled=True)
        partial = jnp.dot(out_grad, panel.T, preferred_element_type=F32).astype(BF16)
        own = lax.psum_scatter(partial, "fsdp", scatter_dimension=1, tiled=True)
        from_them = jnp.zeros_like(own)
    grad_rows = lax.dot_general(
        gathered, out_grad, (((0,), (0,)), ((), ())), preferred_element_type=F32
    ).astype(BF16)
    weight_grad = lax.psum_scatter(grad_rows, "ctx", scatter_dimension=0, tiled=True)
    weight_grad = weight_grad.astype(F32) * (1.0 / math.sqrt(rows * ctx))
    block_out = jnp.dot(gathered, panel, preferred_element_type=F32).astype(BF16)
    pre, end = by_lanes(
        backward_ends, (own, from_them, outer_gate, decay), state_outs, rows, 1
    )
    incoming = prefix(end, decay, rows, True)
    outer_grad, inner_grad, value_grad = by_lanes(
        backward_finish,
        (own, from_them, outer_gate, inner_gate, values, filtered, decay, res, skip, pre, incoming),
        [shape((rows, channels), BF16)] * 3,
        rows,
        2,
    )
    return (block_out, outer_grad, inner_grad, value_grad, weight_grad)


def solution(mesh):
    tile = P("ctx", "fsdp")
    return jax.shard_map(
        shards,
        mesh=mesh,
        in_specs=(tile, tile, tile, tile, P("fsdp"), P("fsdp", None), P("fsdp", None), tile),
        out_specs=(tile,) * 5,
        check_vma=False,
    )
```

```python
import functools
import math

import jax
import jax.numpy as jnp
from jax import lax
from jax.experimental import pallas as pl
from jax.experimental.pallas import tpu as pltpu
from jax.sharding import PartitionSpec as P

F32 = jnp.float32
BF16 = jnp.bfloat16
LANES = 128
SEGS = 8


def rows_at(i, steps):
    return pl.ds(i, SEGS, stride=steps)


def spread(row):
    return jnp.broadcast_to(row, (SEGS, LANES))


def segment_states(u_scr, decay_ref, pre_ref, end_ref, reverse):
    modes = decay_ref.shape[0]
    steps = u_scr.shape[0] // SEGS
    a = [spread(jnp.exp(-decay_ref[r : r + 1, :])) for r in range(modes)]

    def step(k, states):
        i = steps - 1 - k if reverse else k
        u = u_scr[rows_at(i, steps), :]
        return tuple(a[r] * states[r] + u for r in range(modes))

    zero = jnp.zeros((SEGS, LANES), F32)
    states = lax.fori_loop(0, steps, step, (zero,) * modes, unroll=4)
    seg = lax.broadcasted_iota(jnp.int32, (SEGS, LANES), 0)

    def moved(x, by):
        if reverse:
            return jnp.where(seg < SEGS - by, pltpu.roll(x, SEGS - by, 0), 0.0)
        return jnp.where(seg >= by, pltpu.roll(x, by, 0), 0.0)

    last = 0 if reverse else SEGS - 1
    for r in range(modes):
        rate = spread(decay_ref[r : r + 1, :])
        x = states[r]
        for by in (1, 2, 4):
            x = x + jnp.exp(-rate * float(steps * by)) * moved(x, by)
        end_ref[r : r + 1, :] = x[last : last + 1, :]
        pre_ref[r] = moved(x, 1)


def full_scan(u_scr, y_scr, decay_ref, res_ref, pre_ref, incoming_ref, reverse):
    modes = decay_ref.shape[0]
    rows = u_scr.shape[0]
    steps = rows // SEGS
    seg = lax.broadcasted_iota(jnp.int32, (SEGS, LANES), 0)
    ahead = ((SEGS - 1 - seg if reverse else seg) * steps).astype(F32)
    a = []
    first = []
    for r in range(modes):
        rate = spread(decay_ref[r : r + 1, :])
        a.append(jnp.exp(-rate))
        first.append(pre_ref[r] + jnp.exp(-rate * ahead) * incoming_ref[r : r + 1, :])
    res = [spread(res_ref[r : r + 1, :]) for r in range(modes)]

    def step(k, states):
        i = steps - 1 - k if reverse else k
        u = u_scr[rows_at(i, steps), :]
        states = tuple(a[r] * states[r] + u for r in range(modes))
        terms = [res[r] * states[r] for r in range(modes)]
        while len(terms) > 1:
            terms = [p + q for p, q in zip(terms[::2], terms[1::2])]
        y_scr[rows_at(i, steps), :] = terms[0]
        return states

    lax.fori_loop(0, steps, step, tuple(first), unroll=2)


def forward_ends(inner_ref, values_ref, decay_ref, pre_ref, end_ref, u_scr):
    u_scr[...] = inner_ref[...].astype(F32) * values_ref[...].astype(F32)
    segment_states(u_scr, decay_ref, pre_ref, end_ref, False)


def forward_finish(
    inner_ref, values_ref, outer_ref, decay_ref, res_ref, skip_ref, pre_ref, incoming_ref,
    filtered_ref, modulated_ref, u_scr, y_scr,
):
    u_scr[...] = inner_ref[...].astype(F32) * values_ref[...].astype(F32)
    full_scan(u_scr, y_scr, decay_ref, res_ref, pre_ref, incoming_ref, False)
    filtered = y_scr[...] + skip_ref[...] * u_scr[...]
    filtered_ref[...] = filtered
    modulated_ref[...] = (outer_ref[...].astype(F32) * filtered).astype(BF16)


def backward_ends(own_ref, other_ref, outer_ref, decay_ref, pre_ref, end_ref, u_scr):
    grad = own_ref[...].astype(F32) + other_ref[...].astype(F32)
    u_scr[...] = grad * outer_ref[...].astype(F32)
    segment_states(u_scr, decay_ref, pre_ref, end_ref, True)


def backward_finish(
    own_ref, other_ref, outer_ref, inner_ref, values_ref, filtered_ref, decay_ref, res_ref, skip_ref,
    pre_ref, incoming_ref, outer_grad_ref, inner_grad_ref, value_grad_ref, u_scr, y_scr,
):
    grad = own_ref[...].astype(F32) + other_ref[...].astype(F32)
    u_scr[...] = grad * outer_ref[...].astype(F32)
    outer_grad_ref[...] = (grad * filtered_ref[...]).astype(BF16)
    full_scan(u_scr, y_scr, decay_ref, res_ref, pre_ref, incoming_ref, True)
    gated_grad = y_scr[...] + skip_ref[...] * u_scr[...]
    inner_grad_ref[...] = (gated_grad * values_ref[...].astype(F32)).astype(BF16)
    value_grad_ref[...] = (gated_grad * inner_ref[...].astype(F32)).astype(BF16)


def by_lanes(kernel, operands, outs, rows, scans):
    channels = operands[0].shape[-1]

    def spec(x):
        lead = x.shape[:-1]
        return pl.BlockSpec(lead + (LANES,), lambda c, n=len(lead): (0,) * n + (c,))

    work = rows * channels * (24000 if scans > 1 else 16000)
    moved = sum(math.prod(x.shape) * x.dtype.itemsize for x in list(operands) + list(outs))
    return pl.pallas_call(
        kernel,
        grid=(channels // LANES,),
        out_shape=outs,
        in_specs=[spec(x) for x in operands],
        out_specs=[spec(x) for x in outs],
        scratch_shapes=[pltpu.VMEM((rows, LANES), F32)] * scans,
        cost_estimate=pl.CostEstimate(flops=work, bytes_accessed=moved, transcendentals=0),
        name=kernel.__name__,
    )(*operands)


def prefix_kernel(reverse, rows, end_ref, decay_ref, out_ref, sent, got, send_sem, recv_sem):
    me, n = lax.axis_index("ctx"), lax.axis_size("ctx")
    hops = [1 << k for k in range(sent.shape[0])]
    barrier = pltpu.get_barrier_semaphore()
    for hop in hops:
        for peer in (lax.rem(me + hop, n), lax.rem(me + n - hop, n)):
            pl.semaphore_signal(
                barrier, inc=1, device_id={"ctx": peer}, device_id_type=pl.DeviceIdType.MESH
            )
    pl.semaphore_wait(barrier, 2 * len(hops))
    decay = decay_ref[...]
    upto = end_ref[...]
    before = jnp.zeros_like(upto)
    for k, hop in enumerate(hops):
        sent[k] = upto
        copy = pltpu.make_async_remote_copy(
            src_ref=sent.at[k],
            dst_ref=got.at[k],
            send_sem=send_sem.at[k],
            recv_sem=recv_sem.at[k],
            device_id={"ctx": lax.rem(me + (n - hop if reverse else hop), n)},
            device_id_type=pl.DeviceIdType.MESH,
        )
        copy.start()
        near = jnp.exp(-decay * float(rows * (hop - 1)))
        far = jnp.exp(-decay * float(rows * hop))
        copy.wait()
        inside = (me + hop < n) if reverse else (me >= hop)
        term = got[k] * jnp.where(inside, 1.0, 0.0)
        before = before + near * term
        upto = upto + far * term
    out_ref[...] = before


def prefix(end, decay, rows, reverse):
    hops = max(1, (lax.axis_size("ctx") - 1).bit_length())
    whole = pl.BlockSpec(memory_space=pltpu.VMEM)
    return pl.pallas_call(
        functools.partial(prefix_kernel, reverse, rows),
        out_shape=jax.ShapeDtypeStruct(end.shape, F32),
        in_specs=[whole, whole],
        out_specs=whole,
        scratch_shapes=[
            pltpu.VMEM((hops,) + end.shape, F32),
            pltpu.VMEM((hops,) + end.shape, F32),
            pltpu.SemaphoreType.DMA((hops,)),
            pltpu.SemaphoreType.DMA((hops,)),
        ],
        compiler_params=pltpu.CompilerParams(
            collective_id=2 if reverse else 1, has_side_effects=True
        ),
        cost_estimate=pl.CostEstimate(flops=18 * 10**9, bytes_accessed=0, transcendentals=0),
        name="prefix_back" if reverse else "prefix_ahead",
    )(end, decay)


def shards(outer_gate, inner_gate, values, out_weight, skip_gain, residues, decay_rates, out_grad):
    rows, channels = values.shape
    modes = decay_rates.shape[1]
    ctx, fsdp = lax.axis_size("ctx"), lax.axis_size("fsdp")
    at = lax.axis_index("fsdp")
    swap = [(0, 1), (1, 0)]
    shape = jax.ShapeDtypeStruct
    panel = lax.all_gather(out_weight, "ctx", axis=0, tiled=True)
    decay = decay_rates.T
    res = residues.T
    skip = skip_gain[None]
    state_outs = [shape((modes, SEGS, channels), F32), shape((modes, channels), F32)]
    pre, end = by_lanes(forward_ends, (inner_gate, values, decay), state_outs, rows, 1)
    incoming = prefix(end, decay, rows, False)
    filtered, modulated = by_lanes(
        forward_finish,
        (inner_gate, values, outer_gate, decay, res, skip, pre, incoming),
        [shape((rows, channels), F32), shape((rows, channels), BF16)],
        rows,
        2,
    )
    if fsdp == 2:
        other = lax.ppermute(modulated, "fsdp", swap)
        first = jnp.where(at == 0, modulated, other)
        second = jnp.where(at == 0, other, modulated)
        gathered = jnp.concatenate([first, second], axis=1)
        mine = lax.dynamic_slice_in_dim(panel, at * channels, channels, 0)
        theirs = lax.dynamic_slice_in_dim(panel, (1 - at) * channels, channels, 0)
        for_them = jnp.dot(out_grad, theirs.T, preferred_element_type=F32).astype(BF16)
        from_them = lax.ppermute(for_them, "fsdp", swap)
        own = jnp.dot(out_grad, mine.T, preferred_element_type=F32).astype(BF16)
    else:
        gathered = lax.all_gather(modulated, "fsdp", axis=1, tiled=True)
        partial = jnp.dot(out_grad, panel.T, preferred_element_type=F32).astype(BF16)
        own = lax.psum_scatter(partial, "fsdp", scatter_dimension=1, tiled=True)
        from_them = jnp.zeros_like(own)
    grad_rows = lax.dot_general(
        gathered, out_grad, (((0,), (0,)), ((), ())), preferred_element_type=F32
    ).astype(BF16)
    weight_grad = lax.psum_scatter(grad_rows, "ctx", scatter_dimension=0, tiled=True)
    block_out = jnp.dot(gathered, panel, preferred_element_type=F32).astype(BF16)
    pre, end = by_lanes(
        backward_ends, (own, from_them, outer_gate, decay), state_outs, rows, 1
    )
    incoming = prefix(end, decay, rows, True)
    outer_grad, inner_grad, value_grad = by_lanes(
        backward_finish,
        (own, from_them, outer_gate, inner_gate, values, filtered, decay, res, skip, pre, incoming),
        [shape((rows, channels), BF16)] * 3,
        rows,
        2,
    )
    weight_grad, value_grad = lax.optimization_barrier((weight_grad, value_grad))
    weight_grad = weight_grad.astype(F32) * (1.0 / math.sqrt(rows * ctx))
    return (block_out, outer_grad, inner_grad, value_grad, weight_grad)


def solution(mesh):
    tile = P("ctx", "fsdp")
    return jax.shard_map(
        shards,
        mesh=mesh,
        in_specs=(tile, tile, tile, tile, P("fsdp"), P("fsdp", None), P("fsdp", None), tile),
        out_specs=(tile,) * 5,
        check_vma=False,
    )
```

```python
import functools
import math

import jax
import jax.numpy as jnp
from jax import lax
from jax.experimental import pallas as pl
from jax.experimental.pallas import tpu as pltpu
from jax.sharding import PartitionSpec as P

F32 = jnp.float32
BF16 = jnp.bfloat16
LANES = 128
SEGS = 8


def rows_at(i, steps):
    return pl.ds(i, SEGS, stride=steps)


def spread(row):
    return jnp.broadcast_to(row, (SEGS, LANES))


def segment_states(u_scr, decay_ref, pre_ref, end_ref, reverse):
    modes = decay_ref.shape[0]
    steps = u_scr.shape[0] // SEGS
    a = [spread(jnp.exp(-decay_ref[r : r + 1, :])) for r in range(modes)]

    def step(k, states):
        i = steps - 1 - k if reverse else k
        u = u_scr[rows_at(i, steps), :]
        return tuple(a[r] * states[r] + u for r in range(modes))

    zero = jnp.zeros((SEGS, LANES), F32)
    states = lax.fori_loop(0, steps, step, (zero,) * modes, unroll=4)
    seg = lax.broadcasted_iota(jnp.int32, (SEGS, LANES), 0)

    def moved(x, by):
        if reverse:
            return jnp.where(seg < SEGS - by, pltpu.roll(x, SEGS - by, 0), 0.0)
        return jnp.where(seg >= by, pltpu.roll(x, by, 0), 0.0)

    last = 0 if reverse else SEGS - 1
    for r in range(modes):
        rate = spread(decay_ref[r : r + 1, :])
        x = states[r]
        for by in (1, 2, 4):
            x = x + jnp.exp(-rate * float(steps * by)) * moved(x, by)
        end_ref[r : r + 1, :] = x[last : last + 1, :]
        pre_ref[r] = moved(x, 1)


def full_scan(u_scr, y_scr, decay_ref, res_ref, pre_ref, incoming_ref, reverse):
    modes = decay_ref.shape[0]
    rows = u_scr.shape[0]
    steps = rows // SEGS
    seg = lax.broadcasted_iota(jnp.int32, (SEGS, LANES), 0)
    ahead = ((SEGS - 1 - seg if reverse else seg) * steps).astype(F32)
    a = []
    first = []
    for r in range(modes):
        rate = spread(decay_ref[r : r + 1, :])
        a.append(jnp.exp(-rate))
        first.append(pre_ref[r] + jnp.exp(-rate * ahead) * incoming_ref[r : r + 1, :])
    res = [spread(res_ref[r : r + 1, :]) for r in range(modes)]

    def step(k, states):
        i = steps - 1 - k if reverse else k
        u = u_scr[rows_at(i, steps), :]
        states = tuple(a[r] * states[r] + u for r in range(modes))
        terms = [res[r] * states[r] for r in range(modes)]
        while len(terms) > 1:
            terms = [p + q for p, q in zip(terms[::2], terms[1::2])]
        y_scr[rows_at(i, steps), :] = terms[0]
        return states

    lax.fori_loop(0, steps, step, tuple(first), unroll=2)


def forward_ends(inner_ref, values_ref, decay_ref, pre_ref, end_ref, u_scr):
    u_scr[...] = inner_ref[...].astype(F32) * values_ref[...].astype(F32)
    segment_states(u_scr, decay_ref, pre_ref, end_ref, False)


def forward_finish(
    inner_ref, values_ref, outer_ref, decay_ref, res_ref, skip_ref, pre_ref, incoming_ref,
    filtered_ref, modulated_ref, u_scr, y_scr,
):
    u_scr[...] = inner_ref[...].astype(F32) * values_ref[...].astype(F32)
    full_scan(u_scr, y_scr, decay_ref, res_ref, pre_ref, incoming_ref, False)
    filtered = y_scr[...] + skip_ref[...] * u_scr[...]
    filtered_ref[...] = filtered
    modulated_ref[...] = (outer_ref[...].astype(F32) * filtered).astype(BF16)


def backward_ends(own_ref, other_ref, outer_ref, decay_ref, pre_ref, end_ref, u_scr):
    grad = own_ref[...].astype(F32) + other_ref[...].astype(F32)
    u_scr[...] = grad * outer_ref[...].astype(F32)
    segment_states(u_scr, decay_ref, pre_ref, end_ref, True)


def backward_finish(
    own_ref, other_ref, outer_ref, inner_ref, values_ref, filtered_ref, decay_ref, res_ref, skip_ref,
    pre_ref, incoming_ref, outer_grad_ref, inner_grad_ref, value_grad_ref, u_scr, y_scr,
):
    grad = own_ref[...].astype(F32) + other_ref[...].astype(F32)
    u_scr[...] = grad * outer_ref[...].astype(F32)
    outer_grad_ref[...] = (grad * filtered_ref[...]).astype(BF16)
    full_scan(u_scr, y_scr, decay_ref, res_ref, pre_ref, incoming_ref, True)
    gated_grad = y_scr[...] + skip_ref[...] * u_scr[...]
    inner_grad_ref[...] = (gated_grad * values_ref[...].astype(F32)).astype(BF16)
    value_grad_ref[...] = (gated_grad * inner_ref[...].astype(F32)).astype(BF16)


def by_lanes(kernel, operands, outs, rows, scans):
    channels = operands[0].shape[-1]

    def spec(x):
        lead = x.shape[:-1]
        return pl.BlockSpec(lead + (LANES,), lambda c, n=len(lead): (0,) * n + (c,))

    work = rows * channels * (24000 if scans > 1 else 16000)
    moved = sum(math.prod(x.shape) * x.dtype.itemsize for x in list(operands) + list(outs))
    return pl.pallas_call(
        kernel,
        grid=(channels // LANES,),
        out_shape=outs,
        in_specs=[spec(x) for x in operands],
        out_specs=[spec(x) for x in outs],
        scratch_shapes=[pltpu.VMEM((rows, LANES), F32)] * scans,
        cost_estimate=pl.CostEstimate(flops=work, bytes_accessed=moved, transcendentals=0),
        name=kernel.__name__,
    )(*operands)


def prefix_kernel(reverse, rows, end_ref, decay_ref, out_ref, sent, got, send_sem, recv_sem):
    me, n = lax.axis_index("ctx"), lax.axis_size("ctx")
    hops = [1 << k for k in range(sent.shape[0])]
    barrier = pltpu.get_barrier_semaphore()
    for hop in hops:
        for peer in (lax.rem(me + hop, n), lax.rem(me + n - hop, n)):
            pl.semaphore_signal(
                barrier, inc=1, device_id={"ctx": peer}, device_id_type=pl.DeviceIdType.MESH
            )
    pl.semaphore_wait(barrier, 2 * len(hops))
    decay = decay_ref[...]
    upto = end_ref[...]
    before = jnp.zeros_like(upto)
    for k, hop in enumerate(hops):
        sent[k] = upto
        copy = pltpu.make_async_remote_copy(
            src_ref=sent.at[k],
            dst_ref=got.at[k],
            send_sem=send_sem.at[k],
            recv_sem=recv_sem.at[k],
            device_id={"ctx": lax.rem(me + (n - hop if reverse else hop), n)},
            device_id_type=pl.DeviceIdType.MESH,
        )
        copy.start()
        near = jnp.exp(-decay * float(rows * (hop - 1)))
        far = jnp.exp(-decay * float(rows * hop))
        copy.wait()
        inside = (me + hop < n) if reverse else (me >= hop)
        term = got[k] * jnp.where(inside, 1.0, 0.0)
        before = before + near * term
        upto = upto + far * term
    out_ref[...] = before


def prefix(end, decay, rows, reverse):
    hops = max(1, (lax.axis_size("ctx") - 1).bit_length())
    whole = pl.BlockSpec(memory_space=pltpu.VMEM)
    return pl.pallas_call(
        functools.partial(prefix_kernel, reverse, rows),
        out_shape=jax.ShapeDtypeStruct(end.shape, F32),
        in_specs=[whole, whole],
        out_specs=whole,
        scratch_shapes=[
            pltpu.VMEM((hops,) + end.shape, F32),
            pltpu.VMEM((hops,) + end.shape, F32),
            pltpu.SemaphoreType.DMA((hops,)),
            pltpu.SemaphoreType.DMA((hops,)),
        ],
        compiler_params=pltpu.CompilerParams(
            collective_id=2 if reverse else 1, has_side_effects=True
        ),
        cost_estimate=pl.CostEstimate(flops=18 * 10**9, bytes_accessed=0, transcendentals=0),
        name="prefix_back" if reverse else "prefix_ahead",
    )(end, decay)


def shards(outer_gate, inner_gate, values, out_weight, skip_gain, residues, decay_rates, out_grad):
    rows, channels = values.shape
    modes = decay_rates.shape[1]
    ctx, fsdp = lax.axis_size("ctx"), lax.axis_size("fsdp")
    at = lax.axis_index("fsdp")
    swap = [(0, 1), (1, 0)]
    shape = jax.ShapeDtypeStruct
    panel = lax.all_gather(out_weight, "ctx", axis=0, tiled=True)
    decay = decay_rates.T
    res = residues.T
    skip = skip_gain[None]
    state_outs = [shape((modes, SEGS, channels), F32), shape((modes, channels), F32)]
    pre, end = by_lanes(forward_ends, (inner_gate, values, decay), state_outs, rows, 1)
    incoming = prefix(end, decay, rows, False)
    filtered, modulated = by_lanes(
        forward_finish,
        (inner_gate, values, outer_gate, decay, res, skip, pre, incoming),
        [shape((rows, channels), F32), shape((rows, channels), BF16)],
        rows,
        2,
    )
    if fsdp == 2:
        grad_swapped = lax.ppermute(out_grad, "fsdp", swap)
        other = lax.ppermute(modulated, "fsdp", swap)
        first = jnp.where(at == 0, modulated, other)
        second = jnp.where(at == 0, other, modulated)
        gathered = jnp.concatenate([first, second], axis=1)
        mine = lax.dynamic_slice_in_dim(panel, at * channels, channels, 0)
        theirs = lax.dynamic_slice_in_dim(panel, (1 - at) * channels, channels, 0)
        for_them = jnp.dot(out_grad, theirs.T, preferred_element_type=F32).astype(BF16)
        from_them = lax.ppermute(for_them, "fsdp", swap)
        own = jnp.dot(out_grad, mine.T, preferred_element_type=F32).astype(BF16)
    else:
        gathered = lax.all_gather(modulated, "fsdp", axis=1, tiled=True)
        partial = jnp.dot(out_grad, panel.T, preferred_element_type=F32).astype(BF16)
        own = lax.psum_scatter(partial, "fsdp", scatter_dimension=1, tiled=True)
        from_them = jnp.zeros_like(own)
    contract = (((0,), (0,)), ((), ()))
    if fsdp == 2 and ctx % 2 == 0:
        low = jnp.where(at == 0, out_grad, grad_swapped)
        high = jnp.where(at == 0, grad_swapped, out_grad)
        terms = [
            lax.dot_general(modulated, x, contract, preferred_element_type=F32).astype(BF16)
            for x in (low, high)
        ]
        grad_rows = jnp.concatenate(terms, axis=0)
        block = lax.psum_scatter(grad_rows, "ctx", scatter_dimension=0, tiled=True)
        half = ctx // 2
        route = [
            ((p * half + k) * 2 + j, (j * half + k) * 2 + p)
            for p in range(2)
            for k in range(half)
            for j in range(2)
        ]
        weight_grad = block
    else:
        grad_rows = lax.dot_general(
            gathered, out_grad, contract, preferred_element_type=F32
        ).astype(BF16)
        weight_grad = lax.psum_scatter(grad_rows, "ctx", scatter_dimension=0, tiled=True)
    block_out = jnp.dot(gathered, panel, preferred_element_type=F32).astype(BF16)
    pre, end = by_lanes(
        backward_ends, (own, from_them, outer_gate, decay), state_outs, rows, 1
    )
    incoming = prefix(end, decay, rows, True)
    outer_grad, inner_grad, value_grad = by_lanes(
        backward_finish,
        (own, from_them, outer_gate, inner_gate, values, filtered, decay, res, skip, pre, incoming),
        [shape((rows, channels), BF16)] * 3,
        rows,
        2,
    )
    weight_grad, value_grad = lax.optimization_barrier((weight_grad, value_grad))
    if fsdp == 2 and ctx % 2 == 0:
        weight_grad = lax.ppermute(weight_grad, ("ctx", "fsdp"), route)
    weight_grad = weight_grad.astype(F32) * (1.0 / math.sqrt(rows * ctx))
    return (block_out, outer_grad, inner_grad, value_grad, weight_grad)


def solution(mesh):
    tile = P("ctx", "fsdp")
    return jax.shard_map(
        shards,
        mesh=mesh,
        in_specs=(tile, tile, tile, tile, P("fsdp"), P("fsdp", None), P("fsdp", None), tile),
        out_specs=(tile,) * 5,
        check_vma=False,
    )
```

```python
import functools
import math

import jax
import jax.numpy as jnp
from jax import lax
from jax.experimental import pallas as pl
from jax.experimental.pallas import tpu as pltpu
from jax.sharding import PartitionSpec as P

F32 = jnp.float32
BF16 = jnp.bfloat16
LANES = 128
SEGS = 8


def rows_at(i, steps):
    return pl.ds(i, SEGS, stride=steps)


def spread(row):
    return jnp.broadcast_to(row, (SEGS, LANES))


def segment_states(u_scr, decay_ref, pre_ref, end_ref, reverse):
    modes = decay_ref.shape[0]
    steps = u_scr.shape[0] // SEGS
    a = [spread(jnp.exp(-decay_ref[r : r + 1, :])) for r in range(modes)]

    def step(k, states):
        i = steps - 1 - k if reverse else k
        u = u_scr[rows_at(i, steps), :]
        return tuple(a[r] * states[r] + u for r in range(modes))

    zero = jnp.zeros((SEGS, LANES), F32)
    states = lax.fori_loop(0, steps, step, (zero,) * modes, unroll=4)
    seg = lax.broadcasted_iota(jnp.int32, (SEGS, LANES), 0)

    def moved(x, by):
        if reverse:
            return jnp.where(seg < SEGS - by, pltpu.roll(x, SEGS - by, 0), 0.0)
        return jnp.where(seg >= by, pltpu.roll(x, by, 0), 0.0)

    last = 0 if reverse else SEGS - 1
    for r in range(modes):
        rate = spread(decay_ref[r : r + 1, :])
        x = states[r]
        for by in (1, 2, 4):
            x = x + jnp.exp(-rate * float(steps * by)) * moved(x, by)
        end_ref[r : r + 1, :] = x[last : last + 1, :]
        pre_ref[r] = moved(x, 1)


def full_scan(u_scr, y_scr, decay_ref, res_ref, pre_ref, incoming_ref, reverse):
    modes = decay_ref.shape[0]
    rows = u_scr.shape[0]
    steps = rows // SEGS
    seg = lax.broadcasted_iota(jnp.int32, (SEGS, LANES), 0)
    ahead = ((SEGS - 1 - seg if reverse else seg) * steps).astype(F32)
    a = []
    first = []
    for r in range(modes):
        rate = spread(decay_ref[r : r + 1, :])
        a.append(jnp.exp(-rate))
        first.append(pre_ref[r] + jnp.exp(-rate * ahead) * incoming_ref[r : r + 1, :])
    res = [spread(res_ref[r : r + 1, :]) for r in range(modes)]

    def step(k, states):
        i = steps - 1 - k if reverse else k
        u = u_scr[rows_at(i, steps), :]
        states = tuple(a[r] * states[r] + u for r in range(modes))
        terms = [res[r] * states[r] for r in range(modes)]
        while len(terms) > 1:
            terms = [p + q for p, q in zip(terms[::2], terms[1::2])]
        y_scr[rows_at(i, steps), :] = terms[0]
        return states

    lax.fori_loop(0, steps, step, tuple(first), unroll=2)


def forward_ends(inner_ref, values_ref, decay_ref, pre_ref, end_ref, u_scr):
    u_scr[...] = inner_ref[...].astype(F32) * values_ref[...].astype(F32)
    segment_states(u_scr, decay_ref, pre_ref, end_ref, False)


def forward_finish(
    inner_ref, values_ref, outer_ref, decay_ref, res_ref, skip_ref, pre_ref, incoming_ref,
    filtered_ref, modulated_ref, u_scr, y_scr,
):
    u_scr[...] = inner_ref[...].astype(F32) * values_ref[...].astype(F32)
    full_scan(u_scr, y_scr, decay_ref, res_ref, pre_ref, incoming_ref, False)
    filtered = y_scr[...] + skip_ref[...] * u_scr[...]
    filtered_ref[...] = filtered
    modulated_ref[...] = (outer_ref[...].astype(F32) * filtered).astype(BF16)


def backward_ends(own_ref, other_ref, outer_ref, decay_ref, pre_ref, end_ref, u_scr):
    grad = own_ref[...].astype(F32) + other_ref[...].astype(F32)
    u_scr[...] = grad * outer_ref[...].astype(F32)
    segment_states(u_scr, decay_ref, pre_ref, end_ref, True)


def backward_finish(
    own_ref, other_ref, outer_ref, inner_ref, values_ref, filtered_ref, decay_ref, res_ref, skip_ref,
    pre_ref, incoming_ref, outer_grad_ref, inner_grad_ref, value_grad_ref, u_scr, y_scr,
):
    grad = own_ref[...].astype(F32) + other_ref[...].astype(F32)
    u_scr[...] = grad * outer_ref[...].astype(F32)
    outer_grad_ref[...] = (grad * filtered_ref[...]).astype(BF16)
    full_scan(u_scr, y_scr, decay_ref, res_ref, pre_ref, incoming_ref, True)
    gated_grad = y_scr[...] + skip_ref[...] * u_scr[...]
    inner_grad_ref[...] = (gated_grad * values_ref[...].astype(F32)).astype(BF16)
    value_grad_ref[...] = (gated_grad * inner_ref[...].astype(F32)).astype(BF16)


def by_lanes(kernel, operands, outs, rows, scans):
    channels = operands[0].shape[-1]

    def spec(x):
        lead = x.shape[:-1]
        return pl.BlockSpec(lead + (LANES,), lambda c, n=len(lead): (0,) * n + (c,))

    work = rows * channels * (24000 if scans > 1 else 16000)
    moved = sum(math.prod(x.shape) * x.dtype.itemsize for x in list(operands) + list(outs))
    return pl.pallas_call(
        kernel,
        grid=(channels // LANES,),
        out_shape=outs,
        in_specs=[spec(x) for x in operands],
        out_specs=[spec(x) for x in outs],
        scratch_shapes=[pltpu.VMEM((rows, LANES), F32)] * scans,
        cost_estimate=pl.CostEstimate(flops=work, bytes_accessed=moved, transcendentals=0),
        name=kernel.__name__,
    )(*operands)


def prefix_kernel(reverse, rows, end_ref, decay_ref, out_ref, sent, got, send_sem, recv_sem):
    me, n = lax.axis_index("ctx"), lax.axis_size("ctx")
    hops = [1 << k for k in range(sent.shape[0])]
    barrier = pltpu.get_barrier_semaphore()
    for hop in hops:
        for peer in (lax.rem(me + hop, n), lax.rem(me + n - hop, n)):
            pl.semaphore_signal(
                barrier, inc=1, device_id={"ctx": peer}, device_id_type=pl.DeviceIdType.MESH
            )
    pl.semaphore_wait(barrier, 2 * len(hops))
    decay = decay_ref[...]
    upto = end_ref[...]
    before = jnp.zeros_like(upto)
    for k, hop in enumerate(hops):
        sent[k] = upto.astype(BF16)
        copy = pltpu.make_async_remote_copy(
            src_ref=sent.at[k],
            dst_ref=got.at[k],
            send_sem=send_sem.at[k],
            recv_sem=recv_sem.at[k],
            device_id={"ctx": lax.rem(me + (n - hop if reverse else hop), n)},
            device_id_type=pl.DeviceIdType.MESH,
        )
        copy.start()
        near = jnp.exp(-decay * float(rows * (hop - 1)))
        far = jnp.exp(-decay * float(rows * hop))
        copy.wait()
        inside = (me + hop < n) if reverse else (me >= hop)
        term = got[k].astype(F32) * jnp.where(inside, 1.0, 0.0)
        before = before + near * term
        upto = upto + far * term
    out_ref[...] = before


def prefix(end, decay, rows, reverse):
    hops = max(1, (lax.axis_size("ctx") - 1).bit_length())
    whole = pl.BlockSpec(memory_space=pltpu.VMEM)
    return pl.pallas_call(
        functools.partial(prefix_kernel, reverse, rows),
        out_shape=jax.ShapeDtypeStruct(end.shape, F32),
        in_specs=[whole, whole],
        out_specs=whole,
        scratch_shapes=[
            pltpu.VMEM((hops,) + end.shape, BF16),
            pltpu.VMEM((hops,) + end.shape, BF16),
            pltpu.SemaphoreType.DMA((hops,)),
            pltpu.SemaphoreType.DMA((hops,)),
        ],
        compiler_params=pltpu.CompilerParams(
            collective_id=2 if reverse else 1, has_side_effects=True
        ),
        cost_estimate=pl.CostEstimate(flops=18 * 10**9, bytes_accessed=0, transcendentals=0),
        name="prefix_back" if reverse else "prefix_ahead",
    )(end, decay)


def shards(outer_gate, inner_gate, values, out_weight, skip_gain, residues, decay_rates, out_grad):
    rows, channels = values.shape
    modes = decay_rates.shape[1]
    ctx, fsdp = lax.axis_size("ctx"), lax.axis_size("fsdp")
    at = lax.axis_index("fsdp")
    swap = [(0, 1), (1, 0)]
    shape = jax.ShapeDtypeStruct
    panel = lax.all_gather(out_weight, "ctx", axis=0, tiled=True)
    decay = decay_rates.T
    res = residues.T
    skip = skip_gain[None]
    state_outs = [shape((modes, SEGS, channels), F32), shape((modes, channels), F32)]
    pre, end = by_lanes(forward_ends, (inner_gate, values, decay), state_outs, rows, 1)
    incoming = prefix(end, decay, rows, False)
    filtered, modulated = by_lanes(
        forward_finish,
        (inner_gate, values, outer_gate, decay, res, skip, pre, incoming),
        [shape((rows, channels), F32), shape((rows, channels), BF16)],
        rows,
        2,
    )
    if fsdp == 2:
        other = lax.ppermute(modulated, "fsdp", swap)
        first = jnp.where(at == 0, modulated, other)
        second = jnp.where(at == 0, other, modulated)
        gathered = jnp.concatenate([first, second], axis=1)
        mine = lax.dynamic_slice_in_dim(panel, at * channels, channels, 0)
        theirs = lax.dynamic_slice_in_dim(panel, (1 - at) * channels, channels, 0)
        for_them = jnp.dot(out_grad, theirs.T, preferred_element_type=F32).astype(BF16)
        from_them = lax.ppermute(for_them, "fsdp", swap)
        own = jnp.dot(out_grad, mine.T, preferred_element_type=F32).astype(BF16)
    else:
        gathered = lax.all_gather(modulated, "fsdp", axis=1, tiled=True)
        partial = jnp.dot(out_grad, panel.T, preferred_element_type=F32).astype(BF16)
        own = lax.psum_scatter(partial, "fsdp", scatter_dimension=1, tiled=True)
        from_them = jnp.zeros_like(own)
    grad_rows = lax.dot_general(
        gathered, out_grad, (((0,), (0,)), ((), ())), preferred_element_type=F32
    ).astype(BF16)
    weight_grad = lax.psum_scatter(grad_rows, "ctx", scatter_dimension=0, tiled=True)
    block_out = jnp.dot(gathered, panel, preferred_element_type=F32).astype(BF16)
    pre, end = by_lanes(
        backward_ends, (own, from_them, outer_gate, decay), state_outs, rows, 1
    )
    incoming = prefix(end, decay, rows, True)
    outer_grad, inner_grad, value_grad = by_lanes(
        backward_finish,
        (own, from_them, outer_gate, inner_gate, values, filtered, decay, res, skip, pre, incoming),
        [shape((rows, channels), BF16)] * 3,
        rows,
        2,
    )
    weight_grad, value_grad = lax.optimization_barrier((weight_grad, value_grad))
    weight_grad = weight_grad.astype(F32) * (1.0 / math.sqrt(rows * ctx))
    return (block_out, outer_grad, inner_grad, value_grad, weight_grad)


def solution(mesh):
    tile = P("ctx", "fsdp")
    return jax.shard_map(
        shards,
        mesh=mesh,
        in_specs=(tile, tile, tile, tile, P("fsdp"), P("fsdp", None), P("fsdp", None), tile),
        out_specs=(tile,) * 5,
        check_vma=False,
    )
```
